32 devices in a mesh: dp: 16 (over z, y, core), ctx: 2 (over x).
Axes of the slice: x: 2, y: 2, z: 4, core: 2. Of those that a mesh axis runs over, the one named last changes fastest.
Arguments:
- conv_input: bfloat16 [16, 256, 4096], P('dp', 'ctx'), may hold values from -6 to 6
- gate_value: bfloat16 [16, 256, 4096], P('dp', 'ctx'), may hold values from -6 to 6
- out_grad: bfloat16 [16, 256, 4096], P('dp', 'ctx'), may hold values from -6 to 6
- filter_taps: bfloat16 [128, 4096], P('dp'), may hold values from -0.5 to 0.5
Outputs:
- input_grad: bfloat16 [16, 256, 4096], P('dp', 'ctx')
- filter_grad: float32 [128, 4096], P('dp')
The draws below stay inside these ranges and needn't reach their ends.
All inputs are finite; a program needn't handle non-finite values.
Results may differ from the reference program's by a relative error of at most 0.0051.
Values may be sent and summed in bfloat16 or wider, within the bound.
A program may use at most 64 MiB of HBM per device.

```python
import math
import jax
import jax.numpy as jnp
from jax import lax

CHANNELS = 4096
TAPS = 128
SEQ = 256
SEQS = 16
TOKENS = 4096


def level_of(key, dims, pieces, low, high):
    level, own = 1.0, jax.random.fold_in(key, 6)
    for position, parts in pieces:
        steps = jnp.exp(jax.random.uniform(jax.random.fold_in(own, position), (parts,), jnp.float32, low / len(pieces), high / len(pieces)))
        level = level * jnp.repeat(steps, dims[position] // parts).reshape([-1 if axis == position else 1 for axis in range(len(dims))])
    return level


def gaussian(stream_key, dims, width, limit, cuts=(), held_as=jnp.bfloat16):
    array = jax.random.normal(stream_key, dims, jnp.float32) * width
    if len(cuts) > 0:
        array = level_of(stream_key, dims, cuts, -0.22, 0.18) * array
    return jnp.clip(array, min=-limit, max=limit).astype(held_as)


def setup_inputs(seed: int = 0) -> dict:
    arg_keys = jax.random.split(jax.random.key(seed), 5)
    conv_input = gaussian(arg_keys[0], (SEQS, SEQ, CHANNELS), 1.0, 6.0, ((0, 16), (1, 2)))
    gate_value = gaussian(arg_keys[1], (SEQS, SEQ, CHANNELS), 1.0, 6.0, ((0, 16), (1, 2)))
    out_grad = gaussian(arg_keys[2], (SEQS, SEQ, CHANNELS), 1.0, 6.0, ((0, 16), (1, 2)))
    filter_taps = gaussian(arg_keys[3], (TAPS, CHANNELS), TAPS ** -0.5, 0.5, ((0, 16),))
    return dict(conv_input=conv_input, gate_value=gate_value, out_grad=out_grad, filter_taps=filter_taps)


def reference(conv_input, gate_value, out_grad, filter_taps):
    mixed_grad = (out_grad.astype(jnp.float32) * gate_value.astype(jnp.float32)).astype(jnp.bfloat16)
    taps_wide = filter_taps.astype(jnp.float32)

    def one_sequence(pair):
        inputs, mixed = pair
        padded = jnp.concatenate([mixed, jnp.zeros((TAPS - 1, mixed.shape[1]), mixed.dtype)], 0)
        inputs_wide = inputs.astype(jnp.float32)

        def step(index, carry):
            total, grads = carry
            offset = jnp.asarray(index).astype(jnp.int32)
            window = lax.dynamic_slice_in_dim(padded, offset, SEQ, 0).astype(jnp.float32)
            tap_row = lax.dynamic_slice_in_dim(taps_wide, offset, 1, 0)
            total = total + tap_row * window
            grad_row = lax.optimization_barrier(jnp.sum(inputs_wide * window, 0, keepdims=True))
            grads = lax.dynamic_update_slice_in_dim(grads, grad_row, offset, 0)
            return (total, grads)
        start = (jnp.zeros((SEQ, mixed.shape[1]), jnp.float32), jnp.zeros((TAPS, mixed.shape[1]), jnp.float32))
        total, grads = lax.fori_loop(0, TAPS, step, start)
        return (total.astype(jnp.bfloat16), grads)
    input_grad, per_sequence = lax.map(one_sequence, (conv_input, mixed_grad))
    filter_grad = lax.optimization_barrier(jnp.sum(per_sequence, 0)) / math.sqrt(TOKENS)
    return (input_grad, filter_grad)
```

```python
import math

import jax
import jax.numpy as jnp
import numpy as np
from jax import lax
from jax.sharding import PartitionSpec as P


def split(values):
    high = values.astype(jnp.bfloat16)
    return high, (values - high.astype(np.float32)).astype(jnp.bfloat16)


def transforms(length):
    half = length // 2
    angle = np.pi * np.outer(2 * np.arange(half) + 1, np.arange(length)) / length
    forward = np.concatenate([np.cos(angle), -np.sin(angle)], 0)
    inverse = np.concatenate([np.cos(angle), -np.sin(angle)], 0).T / half
    return split(forward.astype(np.float32)), split(inverse.astype(np.float32))


def dot(a, b):
    return lax.dot_general(a, b, (((1,), (0,)), ((), ())), preferred_element_type=jnp.float32)


def shards(conv_input, gate_value, out_grad, filter_taps):
    inputs = conv_input[0]
    rows = inputs.shape[0]
    taps = filter_taps.shape[0] * lax.axis_size("dp")
    (fh, fl), (bh, bl) = transforms(rows + taps)
    half = (rows + taps) // 2
    mixed = (out_grad[0].astype(jnp.float32) * gate_value[0].astype(jnp.float32)).astype(
        jnp.bfloat16
    )
    devices = lax.axis_size("ctx")
    rim = lax.ppermute(mixed[:taps], "ctx", [(i + 1, i) for i in range(devices - 1)])
    full_taps = lax.all_gather(filter_taps, "dp", axis=0, tiled=True)

    def spectrum(x, first=0):
        n = x.shape[0]
        s = dot(fh[:, first : first + n], x) + dot(fl[:, first : first + n], x)
        return s[:half], s[half:]

    def back(re, im, n):
        s = jnp.concatenate([re, im], 0)
        high = s.astype(jnp.bfloat16)
        low = (s - high.astype(jnp.float32)).astype(jnp.bfloat16)
        return dot(bh[:n], high) + dot(bl[:n], high) + dot(bh[:n], low)

    xr, xi = spectrum(inputs)
    gr0, gi0 = spectrum(mixed)
    gr1, gi1 = spectrum(rim, rows)
    gr, gi = gr0 + gr1, gi0 + gi1
    partial = back(xr * gr + xi * gi, xr * gi - xi * gr, taps)
    hr, hi = spectrum(full_taps)
    grad = back(hr * gr + hi * gi, hr * gi - hi * gr, rows)
    shard_grad = lax.psum(lax.psum_scatter(partial, "dp", scatter_dimension=0, tiled=True), "ctx")
    tokens_all = rows * devices * lax.axis_size("dp")
    return (grad.astype(jnp.bfloat16)[None], shard_grad * (1.0 / math.sqrt(tokens_all)))


def solution(mesh):
    in_specs = (P("dp", "ctx", None), P("dp", "ctx", None), P("dp", "ctx", None), P("dp", None))
    out_specs = (P("dp", "ctx", None), P("dp", None))
    return jax.shard_map(shards, mesh=mesh, in_specs=in_specs, out_specs=out_specs, check_vma=False)
```

```python
import functools
import math

import jax
import jax.numpy as jnp
import numpy as np
from jax import lax
from jax.experimental import pallas as pl
from jax.experimental.pallas import tpu as pltpu
from jax.sharding import PartitionSpec as P


def split(values):
    high = values.astype(jnp.bfloat16)
    return high, (values - high.astype(np.float32)).astype(jnp.bfloat16)


def transforms(length):
    half = length // 2
    angle = np.pi * np.outer(2 * np.arange(half) + 1, np.arange(length)) / length
    forward = np.concatenate([np.cos(angle), -np.sin(angle)], 0)
    inverse = np.concatenate([np.cos(angle), -np.sin(angle)], 0).T / half
    return split(forward.astype(np.float32)), split(inverse.astype(np.float32))


def dot(a, b):
    return lax.dot_general(a, b, (((1,), (0,)), ((), ())), preferred_element_type=jnp.float32)


def general(conv_input, gate_value, out_grad, filter_taps):
    inputs = conv_input[0]
    rows = inputs.shape[0]
    taps = filter_taps.shape[0] * lax.axis_size("dp")
    (fh, fl), (bh, bl) = transforms(rows + taps)
    half = (rows + taps) // 2
    mixed = (out_grad[0].astype(jnp.float32) * gate_value[0].astype(jnp.float32)).astype(
        jnp.bfloat16
    )
    devices = lax.axis_size("ctx")
    rim = lax.ppermute(mixed[:taps], "ctx", [(i + 1, i) for i in range(devices - 1)])
    full_taps = lax.all_gather(filter_taps, "dp", axis=0, tiled=True)

    def spectrum(x, first=0):
        n = x.shape[0]
        s = dot(fh[:, first : first + n], x) + dot(fl[:, first : first + n], x)
        return s[:half], s[half:]

    def back(re, im, n):
        s = jnp.concatenate([re, im], 0)
        high = s.astype(jnp.bfloat16)
        low = (s - high.astype(jnp.float32)).astype(jnp.bfloat16)
        return dot(bh[:n], high) + dot(bl[:n], high) + dot(bh[:n], low)

    xr, xi = spectrum(inputs)
    gr0, gi0 = spectrum(mixed)
    gr1, gi1 = spectrum(rim, rows)
    gr, gi = gr0 + gr1, gi0 + gi1
    partial = back(xr * gr + xi * gi, xr * gi - xi * gr, taps)
    hr, hi = spectrum(full_taps)
    grad = back(hr * gr + hi * gi, hr * gi - hi * gr, rows)
    shard_grad = lax.psum(lax.psum_scatter(partial, "dp", scatter_dimension=0, tiled=True), "ctx")
    tokens_all = rows * devices * lax.axis_size("dp")
    return (grad.astype(jnp.bfloat16)[None], shard_grad * (1.0 / math.sqrt(tokens_all)))


CHUNKS = 8
MESH = pl.DeviceIdType.MESH


def kernel(
    pairs, ranks, scale,
    in_hbm, gate_hbm, cot_hbm, taps_hbm, fh, fl, bh, bl,
    out_hbm, fgrad,
    x_in, x_gate, x_cot, g_ext, taps_all, spec, p32, own32, cbuf, csrc, rbuf, sbuf, acc, xbuf, obuf,
    ld_in, ld_gate, ld_cot, ld_taps, st_out,
    rim_s, rim_r, tap_s, tap_f, tap_r, c_s, c_r, s_s, s_r, x_s, x_r,
):
    dp, ctx = lax.axis_index("dp"), lax.axis_index("ctx")
    core, mine = lax.rem(dp, 2), dp // 2
    partner = dp + 1 - 2 * core
    rows, channels = x_in.shape
    wide = channels // CHUNKS
    last = ctx == ranks - 1

    def cols(c):
        return pl.ds(pl.multiple_of(c * wide, wide), wide)

    def load(src, dst, sem, c):
        return pltpu.make_async_copy(src.at[:, cols(c)], dst.at[:, cols(c)], sem.at[c])

    def each(n, body, start=0):
        lax.fori_loop(start, n, lambda i, z: (body(i), z)[1], 0)

    own_taps = pltpu.make_async_copy(taps_hbm, taps_all.at[dp], ld_taps)

    def first_loads(c):
        load(cot_hbm, x_cot, ld_cot, c).start()
        load(gate_hbm, x_gate, ld_gate, c).start()

    each(CHUNKS, first_loads)
    own_taps.start()
    each(CHUNKS, lambda c: load(in_hbm, x_in, ld_in, c).start())

    def peer(k):
        return lax.rem(mine + k, pairs)

    def rank(k):
        return lax.rem(ctx + k, ranks)

    barrier = pltpu.get_barrier_semaphore()
    pl.semaphore_signal(barrier, inc=1, device_id=(partner, ctx), device_id_type=MESH)
    for k in range(1, pairs):
        pl.semaphore_signal(barrier, inc=1, device_id=(2 * peer(k) + core, ctx), device_id_type=MESH)
    for k in range(1, ranks):
        pl.semaphore_signal(barrier, inc=1, device_id=(dp, rank(k)), device_id_type=MESH)
    pl.semaphore_wait(barrier, pairs + ranks - 1)

    def remote(src, dst, send, recv, to):
        return pltpu.make_async_remote_copy(
            src_ref=src, dst_ref=dst, send_sem=send, recv_sem=recv, device_id=to, device_id_type=MESH
        )

    def rim(c):
        return remote(
            g_ext.at[pl.ds(0, rows), cols(c)], g_ext.at[pl.ds(rows, rows), cols(c)],
            rim_s.at[c], rim_r.at[c], (dp, lax.max(ctx - 1, 0)),
        )

    def mix(c):
        load(cot_hbm, x_cot, ld_cot, c).wait()
        load(gate_hbm, x_gate, ld_gate, c).wait()
        a = x_cot[:, cols(c)].astype(jnp.float32)
        b = x_gate[:, cols(c)].astype(jnp.float32)
        g_ext[pl.ds(0, rows), cols(c)] = (a * b).astype(jnp.bfloat16)

        @pl.when(ctx > 0)
        def _():
            rim(c).start()

        @pl.when(last)
        def _():
            g_ext[pl.ds(rows, rows), cols(c)] = jnp.zeros((rows, wide), jnp.bfloat16)

    each(CHUNKS, mix)

    own_taps.wait()

    def tap_send(k):
        return remote(
            taps_all.at[dp], taps_all.at[dp], tap_s.at[k], tap_r.at[dp], (2 * peer(k) + core, ctx)
        )

    def tap_pass(g):
        shard = taps_all.at[2 * g + core]
        return remote(shard, shard, tap_f.at[g], tap_r.at[2 * g + core], (partner, ctx))

    def tap_from(g, c):
        shard = taps_all.at[2 * g + c]
        return remote(shard, shard, tap_f.at[g], tap_r.at[2 * g + c], (partner, ctx))

    each(pairs, lambda k: tap_send(k).start(), 1)
    tap_pass(mine).start()

    def pass_taps():
        def one(k):
            tap_from(peer(k), core).wait_recv()
            tap_pass(peer(k)).start()

        each(pairs, one, 1)

    def all_taps():
        each(pairs, lambda g: tap_from(g, 1 - core).wait_recv())

    def back(value, n):
        high = value.astype(jnp.bfloat16)
        low = (value - high.astype(jnp.float32)).astype(jnp.bfloat16)
        return dot(bh[:n, :], high) + dot(bl[:n, :], high) + dot(bh[:n, :], low)

    half = fh.shape[0] // 2

    def correlate(a, g, n):
        ar, ai, gr, gi = a[:half], a[half:], g[:half], g[half:]
        return back(jnp.concatenate([ar * gr + ai * gi, ar * gi - ai * gr], 0), n)

    count = taps_all.shape[1]
    taps = 2 * pairs * count

    def cross(c):
        return remote(csrc.at[:, :, cols(c)], cbuf.at[:, :, cols(c)], c_s.at[c], c_r.at[c], (partner, ctx))

    def stage1(c):
        @pl.when(jnp.logical_not(last))
        def _():
            rim(c).wait_recv()

        load(in_hbm, x_in, ld_in, c).wait()
        ext = g_ext[:, cols(c)]
        g = dot(fh[...], ext) + dot(fl[...], ext)
        spec[:, cols(c)] = g
        u = x_in[:, cols(c)]
        x = dot(fh[:, :rows], u) + dot(fl[:, :rows], u)
        p32[...] = correlate(x, g, taps).reshape(pairs, 2, count, wide)
        csrc[:, :, cols(c)] = p32[:, 1 - core].astype(jnp.bfloat16)
        own32[:, :, cols(c)] = p32[:, core]
        cross(c).start()

    def scatter(c, k):
        return remote(
            sbuf.at[peer(k), :, cols(c)], rbuf.at[mine, :, cols(c)],
            s_s.at[k, c], s_r.at[mine, c], (2 * peer(k) + core, ctx),
        )

    def scattered(c, k):
        return remote(
            sbuf.at[peer(k), :, cols(c)], rbuf.at[peer(k), :, cols(c)],
            s_s.at[k, c], s_r.at[peer(k), c], (2 * peer(k) + core, ctx),
        )

    def stage2(c):
        cross(c).wait_recv()
        total = own32[:, :, cols(c)] + cbuf[:, :, cols(c)].astype(jnp.float32)
        own32[:, :, cols(c)] = total
        sbuf[:, :, cols(c)] = total.astype(jnp.bfloat16)
        for k in range(1, pairs):
            scatter(c, k).start()

    def swap(c, k):
        return remote(
            xbuf.at[ctx, :, cols(c)], xbuf.at[ctx, :, cols(c)], x_s.at[k, c], x_r.at[ctx, c], (dp, rank(k))
        )

    def swapped(c, k):
        slot = xbuf.at[rank(k), :, cols(c)]
        return remote(slot, slot, x_s.at[k, c], x_r.at[rank(k), c], (dp, rank(k)))

    def stage3(c):
        total = own32[mine, :, cols(c)]
        for k in range(1, pairs):
            scattered(c, k).wait_recv()
            total = total + rbuf[peer(k), :, cols(c)].astype(jnp.float32)
        xbuf[ctx, :, cols(c)] = total.astype(jnp.bfloat16)
        for k in range(1, ranks):
            swap(c, k).start()

    def put(c):
        return pltpu.make_async_copy(obuf.at[:, cols(c)], out_hbm.at[:, cols(c)], st_out.at[c])

    def grad(c):
        t = taps_all[:, :, cols(c)].astype(jnp.float32).reshape(taps, wide).astype(jnp.bfloat16)
        h = dot(fh[:, :taps], t) + dot(fl[:, :taps], t)
        obuf[:, cols(c)] = correlate(h, spec[:, cols(c)], rows).astype(jnp.bfloat16)
        put(c).start()

    middle = CHUNKS // 2

    def step(c):
        stage1(c)

        @pl.when(c >= 1)
        def _():
            stage2(c - 1)

        @pl.when(c >= 2)
        def _():
            stage3(c - 2)

        @pl.when(c == middle - 1)
        def _():
            pass_taps()

        @pl.when(c == middle)
        def _():
            all_taps()

        @pl.when(c >= middle)
        def _():
            each(2 * (c - middle) + 2, grad, 2 * (c - middle))

    each(CHUNKS, step)
    stage2(CHUNKS - 1)
    stage3(CHUNKS - 2)
    stage3(CHUNKS - 1)

    def finish(c):
        for k in range(1, ranks):
            swapped(c, k).wait_recv()
        total = xbuf[0, :, cols(c)].astype(jnp.float32)
        for r in range(1, ranks):
            total = total + xbuf[r, :, cols(c)].astype(jnp.float32)
        fgrad[:, cols(c)] = total * scale

    each(CHUNKS, finish)

    def drain(c):
        put(c).wait()
        cross(c).wait_send()
        for k in range(1, pairs):
            scatter(c, k).wait_send()
        for k in range(1, ranks):
            swap(c, k).wait_send()

        @pl.when(ctx > 0)
        def _():
            rim(c).wait_send()

    each(CHUNKS, drain)
    each(pairs, lambda k: tap_send(k).wait_send(), 1)
    each(pairs, lambda g: tap_pass(g).wait_send())


def shards(conv_input, gate_value, out_grad, filter_taps):
    _, rows, channels = conv_input.shape
    count = filter_taps.shape[0]
    members, ranks = lax.axis_size("dp"), lax.axis_size("ctx")
    taps = count * members
    wide = channels // CHUNKS
    if count % 8 or taps != rows or rows % 16 or members % 2 or channels % (128 * CHUNKS):
        return general(conv_input, gate_value, out_grad, filter_taps)
    pairs = members // 2
    scale = 1.0 / math.sqrt(rows * ranks * members)
    (fh, fl), (bh, bl) = transforms(rows + taps)
    hbm, vmem = pl.BlockSpec(memory_space=pl.ANY), pl.BlockSpec(memory_space=pltpu.VMEM)
    bf, f32, dma = jnp.bfloat16, jnp.float32, pltpu.SemaphoreType.DMA
    out, fgrad = pl.pallas_call(
        functools.partial(kernel, pairs, ranks, scale),
        out_shape=(
            jax.ShapeDtypeStruct((rows, channels), bf),
            jax.ShapeDtypeStruct((count, channels), f32),
        ),
        in_specs=[hbm] * 4 + [vmem] * 4,
        out_specs=(hbm, vmem),
        scratch_shapes=[
            pltpu.VMEM((rows, channels), bf),
            pltpu.VMEM((rows, channels), bf),
            pltpu.VMEM((rows, channels), bf),
            pltpu.VMEM((2 * rows, channels), bf),
            pltpu.VMEM((members, count, channels), bf),
            pltpu.VMEM((rows + taps, channels), f32),
            pltpu.VMEM((pairs, 2, count, wide), f32),
            pltpu.VMEM((pairs, count, channels), f32),
            pltpu.VMEM((pairs, count, channels), bf),
            pltpu.VMEM((pairs, count, channels), bf),
            pltpu.VMEM((pairs, count, channels), bf),
            pltpu.VMEM((pairs, count, channels), bf),
            pltpu.VMEM((count, channels), f32),
            pltpu.VMEM((ranks, count, channels), bf),
            pltpu.VMEM((rows, channels), bf),
            dma((CHUNKS,)), dma((CHUNKS,)), dma((CHUNKS,)), dma, dma((CHUNKS,)),
            dma((CHUNKS,)), dma((CHUNKS,)),
            dma((pairs,)), dma((pairs,)), dma((members,)),
            dma((CHUNKS,)), dma((CHUNKS,)),
            dma((pairs, CHUNKS)), dma((pairs, CHUNKS)),
            dma((ranks, CHUNKS)), dma((ranks, CHUNKS)),
        ],
        compiler_params=pltpu.CompilerParams(
            collective_id=0, has_side_effects=True, vmem_limit_bytes=40 * 2**20
        ),
    )(conv_input[0], gate_value[0], out_grad[0], filter_taps, *map(jnp.asarray, (fh, fl, bh, bl)))
    return out[None], fgrad


def solution(mesh):
    in_specs = (P("dp", "ctx", None), P("dp", "ctx", None), P("dp", "ctx", None), P("dp", None))
    out_specs = (P("dp", "ctx", None), P("dp", None))
    return jax.shard_map(shards, mesh=mesh, in_specs=in_specs, out_specs=out_specs, check_vma=False)
```

```python
import functools
import math

import jax
import jax.numpy as jnp
import numpy as np
from jax import lax
from jax.experimental import pallas as pl
from jax.experimental.pallas import tpu as pltpu
from jax.sharding import PartitionSpec as P


def split(values):
    high = values.astype(jnp.bfloat16)
    return high, (values - high.astype(np.float32)).astype(jnp.bfloat16)


def transforms(length):
    half = length // 2
    angle = np.pi * np.outer(2 * np.arange(half) + 1, np.arange(length)) / length
    forward = np.concatenate([np.cos(angle), -np.sin(angle)], 0)
    inverse = np.concatenate([np.cos(angle), -np.sin(angle)], 0).T / half
    return split(forward.astype(np.float32)), split(inverse.astype(np.float32))


def dot(a, b):
    return lax.dot_general(a, b, (((1,), (0,)), ((), ())), preferred_element_type=jnp.float32)


def general(conv_input, gate_value, out_grad, filter_taps):
    inputs = conv_input[0]
    rows = inputs.shape[0]
    taps = filter_taps.shape[0] * lax.axis_size("dp")
    (fh, fl), (bh, bl) = transforms(rows + taps)
    half = (rows + taps) // 2
    mixed = (out_grad[0].astype(jnp.float32) * gate_value[0].astype(jnp.float32)).astype(
        jnp.bfloat16
    )
    devices = lax.axis_size("ctx")
    rim = lax.ppermute(mixed[:taps], "ctx", [(i + 1, i) for i in range(devices - 1)])
    full_taps = lax.all_gather(filter_taps, "dp", axis=0, tiled=True)

    def spectrum(x, first=0):
        n = x.shape[0]
        s = dot(fh[:, first : first + n], x) + dot(fl[:, first : first + n], x)
        return s[:half], s[half:]

    def back(re, im, n):
        s = jnp.concatenate([re, im], 0)
        high = s.astype(jnp.bfloat16)
        low = (s - high.astype(jnp.float32)).astype(jnp.bfloat16)
        return dot(bh[:n], high) + dot(bl[:n], high) + dot(bh[:n], low)

    xr, xi = spectrum(inputs)
    gr0, gi0 = spectrum(mixed)
    gr1, gi1 = spectrum(rim, rows)
    gr, gi = gr0 + gr1, gi0 + gi1
    partial = back(xr * gr + xi * gi, xr * gi - xi * gr, taps)
    hr, hi = spectrum(full_taps)
    grad = back(hr * gr + hi * gi, hr * gi - hi * gr, rows)
    shard_grad = lax.psum(lax.psum_scatter(partial, "dp", scatter_dimension=0, tiled=True), "ctx")
    tokens_all = rows * devices * lax.axis_size("dp")
    return (grad.astype(jnp.bfloat16)[None], shard_grad * (1.0 / math.sqrt(tokens_all)))


CHUNKS = 8
MESH = pl.DeviceIdType.MESH


def kernel(
    pairs, ranks, scale,
    in_hbm, gate_hbm, cot_hbm, taps_hbm, f_hbm, b_hbm,
    out_hbm, fgrad_hbm,
    x_gate, x_cot, x_ext, g_ext, taps_all, f_all, b_all, p32, own32, csrc, cbuf, half32, ysrc, ybuf,
    zsrc, zbuf, xbuf, obuf, fbuf,
    ld_in, ld_gate, ld_cot, ld_taps, ld_f, st_out, st_f,
    rim_s, rim_r, in_s, in_r, tz_s, ty_s, tc_s, tap_r,
    c_s, c_r, y_s, y_r, z_s, z_r, x_s, x_r,
):
    dp, ctx = lax.axis_index("dp"), lax.axis_index("ctx")
    core, mine = lax.rem(dp, 2), dp // 2
    partner = dp + 1 - 2 * core
    side, place, places = lax.rem(mine, 2), mine // 2, pairs // 2
    across = 2 * (mine + 1 - 2 * side) + core
    rows, channels = x_gate.shape
    wide = channels // CHUNKS
    middle = CHUNKS // 2
    last, first = ctx == ranks - 1, ctx == 0
    left, right = lax.max(ctx - 1, 0), lax.min(ctx + 1, ranks - 1)
    upper, lower = pl.ds(0, rows), pl.ds(rows, rows)

    def cols(c):
        return pl.ds(pl.multiple_of(c * wide, wide), wide)

    def load(src, dst, sem, c):
        return pltpu.make_async_copy(src.at[:, cols(c)], dst.at[:, cols(c)], sem.at[c])

    def load_in(c):
        return pltpu.make_async_copy(in_hbm.at[:, cols(c)], x_ext.at[lower, cols(c)], ld_in.at[c])

    def each(n, body, start=0):
        lax.fori_loop(start, n, lambda i, z: (body(i), z)[1], 0)

    own_taps = pltpu.make_async_copy(taps_hbm, taps_all.at[dp], ld_taps)
    load_f = pltpu.make_async_copy(f_hbm, f_all, ld_f.at[0])
    load_b = pltpu.make_async_copy(b_hbm, b_all, ld_f.at[1])

    def loads(c):
        load(cot_hbm, x_cot, ld_cot, c).start()
        load(gate_hbm, x_gate, ld_gate, c).start()

    each(CHUNKS, loads)
    own_taps.start()
    load_f.start()
    load_b.start()
    each(CHUNKS, lambda c: load_in(c).start())

    def z_peer(k):
        return lax.rem(place + k, places)

    def z_device(k):
        return 4 * z_peer(k) + 2 * side + core

    def rank(k):
        return lax.rem(ctx + k, ranks)

    barrier = pltpu.get_barrier_semaphore()
    pl.semaphore_signal(barrier, inc=1, device_id=(partner, ctx), device_id_type=MESH)
    pl.semaphore_signal(barrier, inc=1, device_id=(across, ctx), device_id_type=MESH)
    for k in range(1, places):
        pl.semaphore_signal(barrier, inc=1, device_id=(z_device(k), ctx), device_id_type=MESH)
    for k in range(1, ranks):
        pl.semaphore_signal(barrier, inc=1, device_id=(dp, rank(k)), device_id_type=MESH)
    pl.semaphore_wait(barrier, places + ranks)

    def remote(src, dst, send, recv, to):
        return pltpu.make_async_remote_copy(
            src_ref=src, dst_ref=dst, send_sem=send, recv_sem=recv, device_id=to, device_id_type=MESH
        )

    def rim(c):
        return remote(g_ext.at[upper, cols(c)], g_ext.at[lower, cols(c)], rim_s.at[c], rim_r.at[c], (dp, left))

    def lend(c):
        return remote(in_hbm.at[:, cols(c)], x_ext.at[upper, cols(c)], in_s.at[c], in_r.at[c], (dp, right))

    def mix(c):
        load(cot_hbm, x_cot, ld_cot, c).wait()
        load(gate_hbm, x_gate, ld_gate, c).wait()
        a = x_cot[:, cols(c)].astype(jnp.float32)
        b = x_gate[:, cols(c)].astype(jnp.float32)
        g_ext[upper, cols(c)] = (a * b).astype(jnp.bfloat16)

        @pl.when(ctx > 0)
        def _():
            rim(c).start()

    @pl.when(jnp.logical_not(last))
    def _():
        each(CHUNKS, lambda c: lend(c).start(), middle)

    each(CHUNKS, mix)

    def shard(p, s, c):
        return taps_all.at[4 * p + 2 * s + c]

    def tap(p, s, c, sem, to):
        return remote(shard(p, s, c), shard(p, s, c), sem, tap_r.at[4 * p + 2 * s + c], (to, ctx))

    def tap_z(k):
        return tap(place, side, core, tz_s.at[k], z_device(k))

    def tap_y(p):
        return tap(p, side, core, ty_s.at[p], across)

    def tap_c(p, s):
        return tap(p, s, core, tc_s.at[p, s], partner)

    def tap_wait(p, s, c):
        tap(p, s, c, ty_s.at[p], partner).wait_recv()

    own_taps.wait()
    each(places, lambda k: tap_z(k).start(), 1)
    tap_y(place).start()
    tap_c(place, side).start()

    def pass_y():
        def one(k):
            tap_wait(z_peer(k), side, core)
            tap_y(z_peer(k)).start()
            tap_c(z_peer(k), side).start()

        each(places, one, 1)

    def pass_c():
        def one(p):
            tap_wait(p, 1 - side, core)
            tap_c(p, 1 - side).start()

        each(places, one)

    def all_taps():
        def one(p):
            tap_wait(p, 0, 1 - core)
            tap_wait(p, 1, 1 - core)

        each(places, one)

    @pl.when(last)
    def _():
        g_ext[lower, :] = jnp.zeros((rows, channels), jnp.bfloat16)

    @pl.when(first)
    def _():
        x_ext[upper, :] = jnp.zeros((rows, channels), jnp.bfloat16)

    load_f.wait()
    load_b.wait()

    def ahead(x):
        n = x.shape[0]
        return dot(f_all[0, :, :n], x) + dot(f_all[1, :, :n], x)

    def later(x):
        return dot(f_all[0, :, rows:], x) + dot(f_all[1, :, rows:], x)

    def back(value, n):
        high = value.astype(jnp.bfloat16)
        low = (value - high.astype(jnp.float32)).astype(jnp.bfloat16)
        return dot(b_all[0, :n, :], high) + dot(b_all[1, :n, :], high) + dot(b_all[0, :n, :], low)

    half = f_all.shape[1] // 2

    def correlate(a, g, n):
        ar, ai, gr, gi = a[:half], a[half:], g[:half], g[half:]
        return back(jnp.concatenate([ar * gr + ai * gi, ar * gi - ai * gr], 0), n)

    count = taps_all.shape[1]
    taps = 2 * pairs * count
    f32, bf = jnp.float32, jnp.bfloat16

    def chunk(i):
        return jnp.where(last, i, lax.rem(i + middle, CHUNKS))

    def cross(c):
        return remote(csrc.at[:, :, cols(c)], cbuf.at[:, :, cols(c)], c_s.at[c], c_r.at[c], (partner, ctx))

    def turn(c):
        return remote(ysrc.at[:, :, cols(c)], ybuf.at[:, :, cols(c)], y_s.at[c], y_r.at[c], (across, ctx))

    def spread(c, k):
        return remote(
            zsrc.at[z_peer(k), :, cols(c)], zbuf.at[place, :, cols(c)],
            z_s.at[k, c], z_r.at[place, c], (z_device(k), ctx),
        )

    def gathered(c, k):
        slot = zbuf.at[z_peer(k), :, cols(c)]
        return remote(slot, slot, z_s.at[k, c], z_r.at[z_peer(k), c], (z_device(k), ctx))

    def swap(c, k):
        slot = xbuf.at[ctx, :, cols(c)]
        return remote(slot, slot, x_s.at[k, c], x_r.at[ctx, c], (dp, rank(k)))

    def swapped(c, k):
        slot = xbuf.at[rank(k), :, cols(c)]
        return remote(slot, slot, x_s.at[k, c], x_r.at[rank(k), c], (dp, rank(k)))

    def stage1(c):
        load_in(c).wait()

        @pl.when(c < middle)
        def _():
            @pl.when(jnp.logical_not(last))
            def _():
                rim(c).wait_recv()

            p = correlate(ahead(x_ext[lower, cols(c)]), ahead(g_ext[:, cols(c)]), taps)
            p32[...] = p.reshape(places, 2, 2, count, wide)

        @pl.when(c >= middle)
        def _():
            @pl.when(jnp.logical_not(first))
            def _():
                lend(c).wait_recv()

            p = correlate(ahead(x_ext[:, cols(c)]), later(g_ext[upper, cols(c)]), taps)
            p32[...] = p.reshape(places, 2, 2, count, wide)

        for s in range(2):
            csrc[pl.ds(s * places, places), :, cols(c)] = p32[:, s, 1 - core].astype(bf)
            own32[pl.ds(s * places, places), :, cols(c)] = p32[:, s, core]
        cross(c).start()

    def stage2(c):
        cross(c).wait_recv()
        there, here = pl.ds((1 - side) * places, places), pl.ds(side * places, places)
        ysrc[:, :, cols(c)] = (own32[there, :, cols(c)] + cbuf[there, :, cols(c)].astype(f32)).astype(bf)
        turn(c).start()
        half32[:, :, cols(c)] = own32[here, :, cols(c)] + cbuf[here, :, cols(c)].astype(f32)

    def stage3(c):
        turn(c).wait_recv()
        total = half32[:, :, cols(c)] + ybuf[:, :, cols(c)].astype(f32)
        half32[:, :, cols(c)] = total
        zsrc[:, :, cols(c)] = total.astype(bf)
        for k in range(1, places):
            spread(c, k).start()

    def stage4(c):
        total = half32[place, :, cols(c)]
        for k in range(1, places):
            gathered(c, k).wait_recv()
            total = total + zbuf[z_peer(k), :, cols(c)].astype(f32)
        xbuf[ctx, :, cols(c)] = total.astype(bf)
        for k in range(1, ranks):
            swap(c, k).start()

    def finish(c):
        for k in range(1, ranks):
            swapped(c, k).wait_recv()
        total = xbuf[0, :, cols(c)].astype(f32)
        for r in range(1, ranks):
            total = total + xbuf[r, :, cols(c)].astype(f32)
        fbuf[:, cols(c)] = total * scale

    def put(c):
        return pltpu.make_async_copy(obuf.at[:, cols(c)], out_hbm.at[:, cols(c)], st_out.at[c])

    put_f = pltpu.make_async_copy(fbuf, fgrad_hbm, st_f)

    def grad(c):
        @pl.when(jnp.logical_and(c >= middle, jnp.logical_not(last)))
        def _():
            rim(c).wait_recv()

        t = taps_all[:, :, cols(c)].astype(f32).reshape(taps, wide).astype(bf)
        obuf[:, cols(c)] = correlate(ahead(t), ahead(g_ext[:, cols(c)]), rows).astype(bf)
        put(c).start()

    def step(i):
        for lag, stage in enumerate((stage1, stage2, stage3, stage4)):
            @pl.when(jnp.logical_and(i >= lag, i < CHUNKS + lag))
            def _(lag=lag, stage=stage):
                stage(chunk(i - lag))

        for when, action in ((2, pass_y), (middle + 1, pass_c), (CHUNKS - 1, all_taps)):
            @pl.when(i == when)
            def _(action=action):
                action()

        @pl.when(i >= CHUNKS - 1)
        def _():
            grad(i - CHUNKS + 1)

        @pl.when(i == CHUNKS + 5)
        def _():
            each(CHUNKS, finish)
            put_f.start()

    each(2 * CHUNKS - 1, step)

    def drain(c):
        put(c).wait()
        cross(c).wait_send()
        turn(c).wait_send()
        for k in range(1, places):
            spread(c, k).wait_send()
        for k in range(1, ranks):
            swap(c, k).wait_send()

        @pl.when(ctx > 0)
        def _():
            rim(c).wait_send()

    each(CHUNKS, drain)

    @pl.when(jnp.logical_not(last))
    def _():
        each(CHUNKS, lambda c: lend(c).wait_send(), middle)

    each(places, lambda k: tap_z(k).wait_send(), 1)

    def drain_taps(p):
        tap_y(p).wait_send()
        tap_c(p, 0).wait_send()
        tap_c(p, 1).wait_send()

    each(places, drain_taps)
    put_f.wait()


def shards(conv_input, gate_value, out_grad, filter_taps):
    _, rows, channels = conv_input.shape
    count = filter_taps.shape[0]
    members, ranks = lax.axis_size("dp"), lax.axis_size("ctx")
    taps = count * members
    wide = channels // CHUNKS
    if count % 8 or taps != rows or rows % 16 or members % 4 or channels % (128 * CHUNKS):
        return general(conv_input, gate_value, out_grad, filter_taps)
    pairs = members // 2
    places = pairs // 2
    scale = 1.0 / math.sqrt(rows * ranks * members)
    forward, inverse = transforms(rows + taps)
    hbm = pl.BlockSpec(memory_space=pl.ANY)
    bf, f32, dma, vmem = jnp.bfloat16, jnp.float32, pltpu.SemaphoreType.DMA, pltpu.VMEM
    out, fgrad = pl.pallas_call(
        functools.partial(kernel, pairs, ranks, scale),
        out_shape=(
            jax.ShapeDtypeStruct((rows, channels), bf),
            jax.ShapeDtypeStruct((count, channels), f32),
        ),
        in_specs=[hbm] * 6,
        out_specs=(hbm, hbm),
        scratch_shapes=[
            vmem((rows, channels), bf),
            vmem((rows, channels), bf),
            vmem((2 * rows, channels), bf),
            vmem((2 * rows, channels), bf),
            vmem((members, count, channels), bf),
            vmem((2, rows + taps, rows + taps), bf),
            vmem((2, rows + taps, rows + taps), bf),
            vmem((places, 2, 2, count, wide), f32),
            vmem((pairs, count, channels), f32),
            vmem((pairs, count, channels), bf),
            vmem((pairs, count, channels), bf),
            vmem((places, count, channels), f32),
            vmem((places, count, channels), bf),
            vmem((places, count, channels), bf),
            vmem((places, count, channels), bf),
            vmem((places, count, channels), bf),
            vmem((ranks, count, channels), bf),
            vmem((rows, channels), bf),
            vmem((count, channels), f32),
            dma((CHUNKS,)), dma((CHUNKS,)), dma((CHUNKS,)), dma, dma((2,)), dma((CHUNKS,)), dma,
            dma((CHUNKS,)), dma((CHUNKS,)), dma((CHUNKS,)), dma((CHUNKS,)),
            dma((places,)), dma((places,)), dma((places, 2)), dma((members,)),
            dma((CHUNKS,)), dma((CHUNKS,)), dma((CHUNKS,)), dma((CHUNKS,)),
            dma((places, CHUNKS)), dma((places, CHUNKS)),
            dma((ranks, CHUNKS)), dma((ranks, CHUNKS)),
        ],
        compiler_params=pltpu.CompilerParams(
            collective_id=0, has_side_effects=True, vmem_limit_bytes=67_000_000
        ),
    )(conv_input[0], gate_value[0], out_grad[0], filter_taps, jnp.asarray(np.stack(forward)), jnp.asarray(np.stack(inverse)))
    return out[None], fgrad


def solution(mesh):
    in_specs = (P("dp", "ctx", None), P("dp", "ctx", None), P("dp", "ctx", None), P("dp", None))
    out_specs = (P("dp", "ctx", None), P("dp", None))
    return jax.shard_map(shards, mesh=mesh, in_specs=in_specs, out_specs=out_specs, check_vma=False)
```

```python
import functools
import math

import jax
import jax.numpy as jnp
import numpy as np
from jax import lax
from jax.experimental import pallas as pl
from jax.experimental.pallas import tpu as pltpu
from jax.sharding import PartitionSpec as P


def split(values):
    high = values.astype(jnp.bfloat16)
    return high, (values - high.astype(np.float32)).astype(jnp.bfloat16)


def transforms(length):
    half = length // 2
    angle = np.pi * np.outer(2 * np.arange(half) + 1, np.arange(length)) / length
    forward = np.concatenate([np.cos(angle), -np.sin(angle)], 0)
    inverse = np.concatenate([np.cos(angle), -np.sin(angle)], 0).T / half
    return split(forward.astype(np.float32)), split(inverse.astype(np.float32))


def dot(a, b):
    return lax.dot_general(a, b, (((1,), (0,)), ((), ())), preferred_element_type=jnp.float32)


def general(conv_input, gate_value, out_grad, filter_taps):
    inputs = conv_input[0]
    rows = inputs.shape[0]
    taps = filter_taps.shape[0] * lax.axis_size("dp")
    (fh, fl), (bh, bl) = transforms(rows + taps)
    half = (rows + taps) // 2
    mixed = (out_grad[0].astype(jnp.float32) * gate_value[0].astype(jnp.float32)).astype(
        jnp.bfloat16
    )
    devices = lax.axis_size("ctx")
    rim = lax.ppermute(mixed[:taps], "ctx", [(i + 1, i) for i in range(devices - 1)])
    full_taps = lax.all_gather(filter_taps, "dp", axis=0, tiled=True)

    def spectrum(x, first=0):
        n = x.shape[0]
        s = dot(fh[:, first : first + n], x) + dot(fl[:, first : first + n], x)
        return s[:half], s[half:]

    def back(re, im, n):
        s = jnp.concatenate([re, im], 0)
        high = s.astype(jnp.bfloat16)
        low = (s - high.astype(jnp.float32)).astype(jnp.bfloat16)
        return dot(bh[:n], high) + dot(bl[:n], high) + dot(bh[:n], low)

    xr, xi = spectrum(inputs)
    gr0, gi0 = spectrum(mixed)
    gr1, gi1 = spectrum(rim, rows)
    gr, gi = gr0 + gr1, gi0 + gi1
    partial = back(xr * gr + xi * gi, xr * gi - xi * gr, taps)
    hr, hi = spectrum(full_taps)
    grad = back(hr * gr + hi * gi, hr * gi - hi * gr, rows)
    shard_grad = lax.psum(lax.psum_scatter(partial, "dp", scatter_dimension=0, tiled=True), "ctx")
    tokens_all = rows * devices * lax.axis_size("dp")
    return (grad.astype(jnp.bfloat16)[None], shard_grad * (1.0 / math.sqrt(tokens_all)))


CHUNKS = 8
MESH = pl.DeviceIdType.MESH


def kernel(
    pairs, ranks, scale,
    in_hbm, gate_hbm, cot_hbm, taps_hbm, f_hbm, b_hbm,
    obuf, fbuf,
    x_gate, x_cot, x_ext, g_ext, taps_all, f_all, b_all, p32, own32, csrc, cbuf, half32, ysrc, ybuf,
    zsrc, zbuf, xbuf,
    ld_in, ld_gate, ld_cot, ld_taps, ld_f,
    rim_s, rim_r, in_s, in_r, tz_s, ty_s, tc_s, tap_r,
    c_s, c_r, y_s, y_r, z_s, z_r, x_s, x_r,
):
    dp, ctx = lax.axis_index("dp"), lax.axis_index("ctx")
    core, mine = lax.rem(dp, 2), dp // 2
    partner = dp + 1 - 2 * core
    side, place, places = lax.rem(mine, 2), mine // 2, pairs // 2
    across = 2 * (mine + 1 - 2 * side) + core
    rows, channels = x_gate.shape
    wide = channels // CHUNKS
    middle = CHUNKS // 2
    last, first = ctx == ranks - 1, ctx == 0
    left, right = lax.max(ctx - 1, 0), lax.min(ctx + 1, ranks - 1)
    upper, lower = pl.ds(0, rows), pl.ds(rows, rows)

    def cols(c):
        return pl.ds(pl.multiple_of(c * wide, wide), wide)

    def load(src, dst, sem, c):
        return pltpu.make_async_copy(src.at[:, cols(c)], dst.at[:, cols(c)], sem.at[c])

    def load_in(c):
        return pltpu.make_async_copy(in_hbm.at[:, cols(c)], x_ext.at[lower, cols(c)], ld_in.at[c])

    def each(n, body, start=0):
        lax.fori_loop(start, n, lambda i, z: (body(i), z)[1], 0)

    own_taps = pltpu.make_async_copy(taps_hbm, taps_all.at[dp], ld_taps)
    load_f = pltpu.make_async_copy(f_hbm, f_all, ld_f.at[0])
    load_b = pltpu.make_async_copy(b_hbm, b_all, ld_f.at[1])

    def loads(c):
        load(cot_hbm, x_cot, ld_cot, c).start()
        load(gate_hbm, x_gate, ld_gate, c).start()

    each(CHUNKS, loads)
    own_taps.start()
    load_f.start()
    load_b.start()
    each(CHUNKS, lambda c: load_in(c).start())

    def z_peer(k):
        return lax.rem(place + k, places)

    def z_device(k):
        return 4 * z_peer(k) + 2 * side + core

    def rank(k):
        return lax.rem(ctx + k, ranks)

    barrier = pltpu.get_barrier_semaphore()
    pl.semaphore_signal(barrier, inc=1, device_id=(partner, ctx), device_id_type=MESH)
    pl.semaphore_signal(barrier, inc=1, device_id=(across, ctx), device_id_type=MESH)
    for k in range(1, places):
        pl.semaphore_signal(barrier, inc=1, device_id=(z_device(k), ctx), device_id_type=MESH)
    for k in range(1, ranks):
        pl.semaphore_signal(barrier, inc=1, device_id=(dp, rank(k)), device_id_type=MESH)
    def remote(src, dst, send, recv, to):
        return pltpu.make_async_remote_copy(
            src_ref=src, dst_ref=dst, send_sem=send, recv_sem=recv, device_id=to, device_id_type=MESH
        )

    def rim(c):
        return remote(g_ext.at[upper, cols(c)], g_ext.at[lower, cols(c)], rim_s.at[c], rim_r.at[c], (dp, left))

    def lend(c):
        return remote(in_hbm.at[:, cols(c)], x_ext.at[upper, cols(c)], in_s.at[c], in_r.at[c], (dp, right))

    def mix(c):
        load(cot_hbm, x_cot, ld_cot, c).wait()
        load(gate_hbm, x_gate, ld_gate, c).wait()
        a = x_cot[:, cols(c)].astype(jnp.float32)
        b = x_gate[:, cols(c)].astype(jnp.float32)
        g_ext[upper, cols(c)] = (a * b).astype(jnp.bfloat16)

    each(middle, mix)
    pl.semaphore_wait(barrier, places + ranks)

    def send_rim(c):
        @pl.when(ctx > 0)
        def _():
            rim(c).start()

    each(middle, send_rim)

    @pl.when(jnp.logical_not(last))
    def _():
        each(CHUNKS, lambda c: lend(c).start(), middle)

    each(CHUNKS, lambda c: (mix(c), send_rim(c)), middle)

    def shard(p, s, c):
        return taps_all.at[4 * p + 2 * s + c]

    def tap(p, s, c, sem, to):
        return remote(shard(p, s, c), shard(p, s, c), sem, tap_r.at[4 * p + 2 * s + c], (to, ctx))

    def tap_z(k):
        return tap(place, side, core, tz_s.at[k], z_device(k))

    def tap_y(p):
        return tap(p, side, core, ty_s.at[p], across)

    def tap_c(p, s):
        return tap(p, s, core, tc_s.at[p, s], partner)

    def tap_wait(p, s, c):
        tap(p, s, c, ty_s.at[p], partner).wait_recv()

    own_taps.wait()
    each(places, lambda k: tap_z(k).start(), 1)
    tap_y(place).start()
    tap_c(place, side).start()

    def pass_y():
        def one(k):
            tap_wait(z_peer(k), side, core)
            tap_y(z_peer(k)).start()
            tap_c(z_peer(k), side).start()

        each(places, one, 1)

    def pass_c():
        def one(p):
            tap_wait(p, 1 - side, core)
            tap_c(p, 1 - side).start()

        each(places, one)

    def all_taps():
        def one(p):
            tap_wait(p, 0, 1 - core)
            tap_wait(p, 1, 1 - core)

        each(places, one)

    @pl.when(last)
    def _():
        g_ext[lower, :] = jnp.zeros((rows, channels), jnp.bfloat16)

    @pl.when(first)
    def _():
        x_ext[upper, :] = jnp.zeros((rows, channels), jnp.bfloat16)

    load_f.wait()
    load_b.wait()

    def ahead(x):
        n = x.shape[0]
        return dot(f_all[0, :, :n], x) + dot(f_all[1, :, :n], x)

    def later(x):
        return dot(f_all[0, :, rows:], x) + dot(f_all[1, :, rows:], x)

    def back(value, n):
        high = value.astype(jnp.bfloat16)
        low = (value - high.astype(jnp.float32)).astype(jnp.bfloat16)
        return dot(b_all[0, :n, :], high) + dot(b_all[1, :n, :], high) + dot(b_all[0, :n, :], low)

    half = f_all.shape[1] // 2

    def correlate(a, g, n):
        ar, ai, gr, gi = a[:half], a[half:], g[:half], g[half:]
        return back(jnp.concatenate([ar * gr + ai * gi, ar * gi - ai * gr], 0), n)

    count = taps_all.shape[1]
    taps = 2 * pairs * count
    f32, bf = jnp.float32, jnp.bfloat16

    def chunk(i):
        return jnp.where(last, i, lax.rem(i + middle, CHUNKS))

    def cross(c):
        return remote(csrc.at[:, :, cols(c)], cbuf.at[:, :, cols(c)], c_s.at[c], c_r.at[c], (partner, ctx))

    def turn(c):
        return remote(ysrc.at[:, :, cols(c)], ybuf.at[:, :, cols(c)], y_s.at[c], y_r.at[c], (across, ctx))

    def spread(c, k):
        return remote(
            zsrc.at[z_peer(k), :, cols(c)], zbuf.at[place, :, cols(c)],
            z_s.at[k, c], z_r.at[place, c], (z_device(k), ctx),
        )

    def gathered(c, k):
        slot = zbuf.at[z_peer(k), :, cols(c)]
        return remote(slot, slot, z_s.at[k, c], z_r.at[z_peer(k), c], (z_device(k), ctx))

    def swap(c, k):
        slot = xbuf.at[ctx, :, cols(c)]
        return remote(slot, slot, x_s.at[k, c], x_r.at[ctx, c], (dp, rank(k)))

    def swapped(c, k):
        slot = xbuf.at[rank(k), :, cols(c)]
        return remote(slot, slot, x_s.at[k, c], x_r.at[rank(k), c], (dp, rank(k)))

    def stage1(c):
        load_in(c).wait()

        @pl.when(c < middle)
        def _():
            @pl.when(jnp.logical_not(last))
            def _():
                rim(c).wait_recv()

            p = correlate(ahead(x_ext[lower, cols(c)]), ahead(g_ext[:, cols(c)]), taps)
            p32[...] = p.reshape(places, 2, 2, count, wide)

        @pl.when(c >= middle)
        def _():
            @pl.when(jnp.logical_not(first))
            def _():
                lend(c).wait_recv()

            p = correlate(ahead(x_ext[:, cols(c)]), later(g_ext[upper, cols(c)]), taps)
            p32[...] = p.reshape(places, 2, 2, count, wide)

        for s in range(2):
            csrc[pl.ds(s * places, places), :, cols(c)] = p32[:, s, 1 - core].astype(bf)
            own32[pl.ds(s * places, places), :, cols(c)] = p32[:, s, core]
        cross(c).start()

    def stage2(c):
        cross(c).wait_recv()
        there, here = pl.ds((1 - side) * places, places), pl.ds(side * places, places)
        ysrc[:, :, cols(c)] = (own32[there, :, cols(c)] + cbuf[there, :, cols(c)].astype(f32)).astype(bf)
        turn(c).start()
        half32[:, :, cols(c)] = own32[here, :, cols(c)] + cbuf[here, :, cols(c)].astype(f32)

    def stage3(c):
        turn(c).wait_recv()
        total = half32[:, :, cols(c)] + ybuf[:, :, cols(c)].astype(f32)
        half32[:, :, cols(c)] = total
        zsrc[:, :, cols(c)] = total.astype(bf)
        for k in range(1, places):
            spread(c, k).start()

    def stage4(c):
        total = half32[place, :, cols(c)]
        for k in range(1, places):
            gathered(c, k).wait_recv()
            total = total + zbuf[z_peer(k), :, cols(c)].astype(f32)
        xbuf[ctx, :, cols(c)] = total.astype(bf)
        for k in range(1, ranks):
            swap(c, k).start()

    def finish(c):
        for k in range(1, ranks):
            swapped(c, k).wait_recv()
        total = xbuf[0, :, cols(c)].astype(f32)
        for r in range(1, ranks):
            total = total + xbuf[r, :, cols(c)].astype(f32)
        fbuf[:, cols(c)] = total * scale

    def grad(c):
        @pl.when(jnp.logical_and(c >= middle, jnp.logical_not(last)))
        def _():
            rim(c).wait_recv()

        t = taps_all[:, :, cols(c)].astype(f32).reshape(taps, wide).astype(bf)
        obuf[:, cols(c)] = correlate(ahead(t), ahead(g_ext[:, cols(c)]), rows).astype(bf)

    def step(i):
        for lag, stage in list(zip((0, 1, 3, 5), (stage1, stage2, stage3, stage4))):
            @pl.when(jnp.logical_and(i >= lag, i < CHUNKS + lag))
            def _(lag=lag, stage=stage):
                stage(chunk(i - lag))

        for when, action in ((2, pass_y), (middle + 1, pass_c), (CHUNKS - 1, all_taps)):
            @pl.when(i == when)
            def _(action=action):
                action()

        @pl.when(i >= CHUNKS - 1)
        def _():
            grad(i - CHUNKS + 1)

        @pl.when(i == 2 * CHUNKS - 2)
        def _():
            each(CHUNKS, finish)

    each(2 * CHUNKS - 1, step)

    def drain(c):
        cross(c).wait_send()
        turn(c).wait_send()
        for k in range(1, places):
            spread(c, k).wait_send()
        for k in range(1, ranks):
            swap(c, k).wait_send()

        @pl.when(ctx > 0)
        def _():
            rim(c).wait_send()

    each(CHUNKS, drain)

    @pl.when(jnp.logical_not(last))
    def _():
        each(CHUNKS, lambda c: lend(c).wait_send(), middle)

    each(places, lambda k: tap_z(k).wait_send(), 1)

    def drain_taps(p):
        tap_y(p).wait_send()
        tap_c(p, 0).wait_send()
        tap_c(p, 1).wait_send()

    each(places, drain_taps)


def shards(conv_input, gate_value, out_grad, filter_taps):
    _, rows, channels = conv_input.shape
    count = filter_taps.shape[0]
    members, ranks = lax.axis_size("dp"), lax.axis_size("ctx")
    taps = count * members
    wide = channels // CHUNKS
    if count % 8 or taps != rows or rows % 16 or members % 4 or channels % (128 * CHUNKS):
        return general(conv_input, gate_value, out_grad, filter_taps)
    pairs = members // 2
    places = pairs // 2
    scale = 1.0 / math.sqrt(rows * ranks * members)
    forward, inverse = transforms(rows + taps)
    hbm = pl.BlockSpec(memory_space=pl.ANY)
    bf, f32, dma, vmem = jnp.bfloat16, jnp.float32, pltpu.SemaphoreType.DMA, pltpu.VMEM
    out, fgrad = pl.pallas_call(
        functools.partial(kernel, pairs, ranks, scale),
        out_shape=(
            jax.ShapeDtypeStruct((rows, channels), bf),
            jax.ShapeDtypeStruct((count, channels), f32),
        ),
        in_specs=[hbm] * 6,
        out_specs=(pl.BlockSpec(memory_space=vmem),) * 2,
        scratch_shapes=[
            vmem((rows, channels), bf),
            vmem((rows, channels), bf),
            vmem((2 * rows, channels), bf),
            vmem((2 * rows, channels), bf),
            vmem((members, count, channels), bf),
            vmem((2, rows + taps, rows + taps), bf),
            vmem((2, rows + taps, rows + taps), bf),
            vmem((places, 2, 2, count, wide), f32),
            vmem((pairs, count, channels), f32),
            vmem((pairs, count, channels), bf),
            vmem((pairs, count, channels), bf),
            vmem((places, count, channels), f32),
            vmem((places, count, channels), bf),
            vmem((places, count, channels), bf),
            vmem((places, count, channels), bf),
            vmem((places, count, channels), bf),
            vmem((ranks, count, channels), bf),
            dma((CHUNKS,)), dma((CHUNKS,)), dma((CHUNKS,)), dma, dma((2,)),
            dma((CHUNKS,)), dma((CHUNKS,)), dma((CHUNKS,)), dma((CHUNKS,)),
            dma((places,)), dma((places,)), dma((places, 2)), dma((members,)),
            dma((CHUNKS,)), dma((CHUNKS,)), dma((CHUNKS,)), dma((CHUNKS,)),
            dma((places, CHUNKS)), dma((places, CHUNKS)),
            dma((ranks, CHUNKS)), dma((ranks, CHUNKS)),
        ],
        compiler_params=pltpu.CompilerParams(
            collective_id=0, has_side_effects=True, vmem_limit_bytes=65_900_000
        ),
    )(conv_input[0], gate_value[0], out_grad[0], filter_taps, jnp.asarray(np.stack(forward)), jnp.asarray(np.stack(inverse)))
    return out[None], fgrad


def solution(mesh):
    in_specs = (P("dp", "ctx", None), P("dp", "ctx", None), P("dp", "ctx", None), P("dp", None))
    out_specs = (P("dp", "ctx", None), P("dp", None))
    return jax.shard_map(shards, mesh=mesh, in_specs=in_specs, out_specs=out_specs, check_vma=False)
```
